32 devices in a mesh: dp: 16 (over z, y, core), seq: 2 (over x).
Axes of the slice: x: 2, y: 2, z: 4, core: 2. Of those that a mesh axis runs over, the one named last changes fastest.
Arguments:
- inputs: float32 [16, 256, 640], P('dp', 'seq'), may hold values from -6 to 6
- positions: int32 [16, 256], P('dp'), may hold values from 0 to 1277, as said below
- cotangent: float32 [16, 256, 640], P('dp', 'seq'), may hold values from -16 to 16
- q_weight: bfloat16 [1024, 640], P(('dp', 'seq')), may hold values from -0.5 to 0.5
- k_weight: bfloat16 [256, 640], P(('dp', 'seq')), may hold values from -0.5 to 0.5
- v_weight: bfloat16 [256, 640], P(('dp', 'seq')), may hold values from -0.25 to 0.25
- o_weight: bfloat16 [1024, 640], P(('dp', 'seq')), may hold values from -0.1875 to 0.1875
- gate_weight: bfloat16 [2048, 640], P(('dp', 'seq')), may hold values from -0.25 to 0.25
- up_weight: bfloat16 [2048, 640], P(('dp', 'seq')), may hold values from -0.25 to 0.25
- down_weight: bfloat16 [2048, 640], P(('dp', 'seq')), may hold values from -0.125 to 0.125
- norm_gains: bfloat16 [3072], P(('dp', 'seq')), may hold values from 0.5 to 1.5
Outputs:
- output: float32 [16, 256, 640], P('dp', 'seq')
- input_grad: float32 [16, 256, 640], P('dp', 'seq')
- q_grad: float32 [1024, 640], P(('dp', 'seq'))
- k_grad: float32 [256, 640], P(('dp', 'seq'))
- v_grad: float32 [256, 640], P(('dp', 'seq'))
- o_grad: float32 [1024, 640], P(('dp', 'seq'))
- gate_grad: float32 [2048, 640], P(('dp', 'seq'))
- up_grad: float32 [2048, 640], P(('dp', 'seq'))
- down_grad: float32 [2048, 640], P(('dp', 'seq'))
- gains_grad: float32 [3072], P(('dp', 'seq'))
The draws below stay inside these ranges and needn't reach their ends.
Inputs may be any that keep to these rules, and one draw needn't show every extreme that they name: Along a row, positions rise by one from token to token, except where a new document begins and they restart at 0; every row has at least one such restart after its first token.
All inputs are finite; a program needn't handle non-finite values.
Results may differ from the reference program's by a relative error of at most 0.014.
Values may be sent and summed in bfloat16 or wider, within the bound.
A program may use at most 128 MiB of HBM per device.

```python
import jax
import jax.numpy as jnp
from jax import lax

D = 640
HQ = 4
HD = 256
FF = 2048
WIN = 512
SEQ_LEN = 256
SEQS = 16


def draw_positions(key, part):
    key_break, key_extra, key_offset = jax.random.split(key, 3)
    steps_row = jnp.arange(SEQ_LEN, dtype=jnp.int32)[None, :]
    row_ids = jnp.arange(SEQS, dtype=jnp.int32)[:, None]
    breaks = jax.random.randint(key_break, (SEQS, 1), 1, SEQ_LEN)
    breaks = jnp.where(row_ids == 0, SEQ_LEN - 1, breaks)
    extra = jax.random.randint(key_extra, (SEQS, SEQ_LEN), 0, 2 * SEQ_LEN) == 0
    extra = extra & (row_ids != 0)
    offset = jax.random.randint(key_offset, (SEQS, 1), 0, 2 * WIN)
    offset = jnp.where(row_ids == 0, 2 * WIN - 1, offset)
    starts = (steps_row == breaks) | extra
    marked = jnp.where(starts, steps_row, -1)
    latest = lax.cummax(marked, axis=1)
    return jnp.where(latest >= 0, steps_row - latest, steps_row + offset).astype(jnp.int32)


def draw_norm_gains(key, part):
    total = 4 * D + 2 * HD
    return jax.random.uniform(key, (total,), jnp.float32, 0.5, 1.5).astype(jnp.bfloat16)


def draw_cotangent(key, part):
    key_vals, key_rows = jax.random.split(key, 2)
    rising = 3.0 ** (jnp.arange(SEQS, dtype=jnp.float32) / max(SEQS - 1, 1))
    jitter = jax.random.uniform(key_rows, (SEQS,), jnp.float32, 0.7, 1.3)
    scales = (rising * jitter)[:, None, None]
    values = jnp.clip(jax.random.normal(key_vals, (SEQS, SEQ_LEN, D), jnp.float32), -4.0, 4.0)
    return values * scales


def draw_inputs(key, part):
    return jnp.clip(jax.random.normal(key, (SEQS, SEQ_LEN, D), jnp.float32), -6.0, 6.0)


def projection_draw(key, rows):
    values = jax.random.normal(key, (rows, D), jnp.float32)
    return jnp.clip(values * D ** (-0.5), -0.5, 0.5)


def draw_k_weight(key, part):
    return projection_draw(jax.random.fold_in(key, 11), HD).astype(jnp.bfloat16)


def draw_q_weight(key, part):
    return projection_draw(jax.random.fold_in(key, 12), HQ * HD).astype(jnp.bfloat16)


def block_scale(own_key, extent, pieces, low, top_value):
    level, own = 1.0, jax.random.fold_in(own_key, 6)
    for position, shards_of in pieces:
        heights = jnp.exp(jax.random.uniform(jax.random.fold_in(own, position), (shards_of,), jnp.float32, low / len(pieces), top_value / len(pieces)))
        level = level * jnp.repeat(heights, extent[position] // shards_of).reshape([-1 if axis == position else 1 for axis in range(len(extent))])
    return level


def bell_draw(own_key, shape, width, most, cuts=(), kind=jnp.bfloat16):
    values = jax.random.normal(own_key, shape, jnp.float32) * width
    if len(cuts) > 0:
        values = block_scale(own_key, shape, cuts, -0.22, 0.18) * values
    return jnp.clip(values, min=-most, max=most).astype(kind)


def setup_inputs(seed: int = 0) -> dict:
    seeds = jax.random.split(jax.random.key(seed), 12)
    return {
        "inputs": draw_inputs(jax.random.fold_in(seeds[11], 71), 0),
        "positions": draw_positions(jax.random.fold_in(seeds[11], 71), 0),
        "cotangent": draw_cotangent(jax.random.fold_in(seeds[11], 71), 0),
        "q_weight": draw_q_weight(jax.random.fold_in(seeds[11], 71), 0),
        "k_weight": draw_k_weight(jax.random.fold_in(seeds[11], 71), 0),
        "v_weight": bell_draw(seeds[5], (HD, D), D ** -0.5, 0.25, ((0, 32),)),
        "o_weight": bell_draw(seeds[6], (HQ * HD, D), (HQ * HD) ** -0.5, 0.1875, ((0, 32),)),
        "gate_weight": bell_draw(seeds[7], (FF, D), D ** -0.5, 0.25, ((0, 32),)),
        "up_weight": bell_draw(seeds[8], (FF, D), D ** -0.5, 0.25, ((0, 32),)),
        "down_weight": bell_draw(seeds[9], (FF, D), FF ** -0.5, 0.125, ((0, 32),)),
        "norm_gains": draw_norm_gains(jax.random.fold_in(seeds[11], 71), 0),
    }


EPSILON = 1e-06

def rms_scale(values, scales):
    inverse = lax.rsqrt(lax.optimization_barrier(jnp.mean(values * values, axis=-1, keepdims=True)) + EPSILON)
    return values * inverse * scales

def rotary_tables(positions):
    half_size = HD // 2
    frequency = 10000.0 ** (-2.0 * jnp.arange(half_size, dtype=jnp.float32) / HD)
    angles = positions.astype(jnp.float32)[:, None] * frequency[None, :]
    angles = jnp.concatenate([angles, angles], axis=-1)
    return (jnp.cos(angles), jnp.sin(angles))

def norm_rotate(raw_values, scales, cos_table, sin_table):
    normed = rms_scale(raw_values, scales)
    front_half = normed[..., :HD // 2]
    back_half = normed[..., HD // 2:]
    turned = jnp.concatenate([-back_half, front_half], axis=-1)
    return normed * cos_table[:, None, :] + turned * sin_table[:, None, :]

def window_mask(query_pos, key_pos, query_idx, key_idx):
    spacing = query_pos[:, None] - key_pos[None, :]
    return (spacing == query_idx[:, None] - key_idx[None, :]) & (spacing >= 0) & (spacing < WIN)

def glu_product(gate_pre, up_pre):
    return jax.nn.gelu(gate_pre, approximate=True) * up_pre

def split_gains(gains_all):
    return (gains_all[0:D], gains_all[D:2 * D], gains_all[2 * D:3 * D], gains_all[3 * D:4 * D], gains_all[4 * D:4 * D + HD], gains_all[4 * D + HD:4 * D + 2 * HD])

def one_sequence(seq_inputs, seq_cotangent, seq_positions, weights, gains_all):
    w_query, w_key, w_value, w_out, w_gate, w_upper, w_down = weights
    gain_in, gain_attn, gain_pre, gain_post, gain_query, gain_key = split_gains(gains_all)
    length = seq_inputs.shape[0]
    scale = HD ** (-0.5)
    cos_table, sin_table = rotary_tables(seq_positions)
    token_idx = jnp.arange(length, dtype=jnp.int32)
    allowed = window_mask(seq_positions, seq_positions, token_idx, token_idx)
    normed_in = rms_scale(seq_inputs, gain_in).astype(jnp.bfloat16)
    queries_raw = jnp.dot(normed_in, w_query.T, preferred_element_type=jnp.float32).reshape(length, HQ, HD)
    keys_raw = jnp.dot(normed_in, w_key.T, preferred_element_type=jnp.float32).reshape(length, 1, HD)
    values_raw = jnp.dot(normed_in, w_value.T, preferred_element_type=jnp.float32)
    queries_rot = norm_rotate(queries_raw, gain_query, cos_table, sin_table).astype(jnp.bfloat16)
    keys_rot = norm_rotate(keys_raw, gain_key, cos_table, sin_table)[:, 0].astype(jnp.bfloat16)
    values_b = values_raw.astype(jnp.bfloat16)
    query_heads = jnp.transpose(queries_rot, (1, 0, 2))
    scores = scale * jnp.einsum('hqd,kd->hqk', query_heads.astype(jnp.float32), keys_rot.astype(jnp.float32))
    scores = jnp.where(allowed[None], scores, -1e+30)
    highest = lax.optimization_barrier(jnp.max(scores, axis=-1, keepdims=True))
    log_total = highest + jnp.log(lax.optimization_barrier(jnp.sum(jnp.exp(scores - highest), axis=-1, keepdims=True)))
    probs = jnp.exp(scores - log_total)
    probs_b = probs.astype(jnp.bfloat16)
    attended = jnp.einsum('hqk,kd->hqd', probs_b.astype(jnp.float32), values_b.astype(jnp.float32)).astype(jnp.bfloat16)
    merged = jnp.transpose(attended, (1, 0, 2)).reshape(length, HQ * HD)
    branch = jnp.dot(merged, w_out, preferred_element_type=jnp.float32)
    middle = seq_inputs + rms_scale(branch, gain_attn)
    normed_ff = rms_scale(middle, gain_pre).astype(jnp.bfloat16)
    gate_pre = jnp.dot(normed_ff, w_gate.T, preferred_element_type=jnp.float32)
    up_pre = jnp.dot(normed_ff, w_upper.T, preferred_element_type=jnp.float32)
    hidden = glu_product(gate_pre, up_pre).astype(jnp.bfloat16)
    ffn_out = jnp.dot(hidden, w_down, preferred_element_type=jnp.float32)
    output = middle + rms_scale(ffn_out, gain_post)
    unused, pull = jax.vjp(rms_scale, ffn_out, gain_post)
    d_ffn, grad_post = pull(seq_cotangent)
    d_ffn = d_ffn.astype(jnp.bfloat16)
    down_grad = jnp.dot(hidden.T, d_ffn, preferred_element_type=jnp.float32)
    d_hidden = jnp.dot(d_ffn, w_down.T, preferred_element_type=jnp.float32)
    unused, pull = jax.vjp(glu_product, gate_pre, up_pre)
    d_gate, d_up = pull(d_hidden)
    d_gate = d_gate.astype(jnp.bfloat16)
    d_up = d_up.astype(jnp.bfloat16)
    gate_grad = jnp.dot(d_gate.T, normed_ff, preferred_element_type=jnp.float32)
    up_grad = jnp.dot(d_up.T, normed_ff, preferred_element_type=jnp.float32)
    d_normed_ff = jnp.dot(d_gate, w_gate, preferred_element_type=jnp.float32) + jnp.dot(d_up, w_upper, preferred_element_type=jnp.float32)
    unused, pull = jax.vjp(rms_scale, middle, gain_pre)
    d_mid_norm, grad_pre = pull(d_normed_ff)
    d_middle = seq_cotangent + d_mid_norm
    unused, pull = jax.vjp(rms_scale, branch, gain_attn)
    d_branch, grad_attn = pull(d_middle)
    d_branch = d_branch.astype(jnp.bfloat16)
    o_grad = jnp.dot(merged.T, d_branch, preferred_element_type=jnp.float32)
    d_merged = jnp.dot(d_branch, w_out.T, preferred_element_type=jnp.float32).astype(jnp.bfloat16)
    d_heads = jnp.transpose(d_merged.reshape(length, HQ, HD), (1, 0, 2)).astype(jnp.float32)
    delta = lax.optimization_barrier(jnp.sum(d_heads * attended.astype(jnp.float32), axis=-1, keepdims=True))
    d_probs = jnp.einsum('hqd,kd->hqk', d_heads, values_b.astype(jnp.float32))
    d_scores = (probs * (d_probs - delta)).astype(jnp.bfloat16).astype(jnp.float32)
    d_queries_rot = scale * jnp.einsum('hqk,kd->hqd', d_scores, keys_rot.astype(jnp.float32))
    d_keys_rot = scale * jnp.einsum('hqk,hqd->kd', d_scores, query_heads.astype(jnp.float32))
    d_values = jnp.einsum('hqk,hqd->kd', probs_b.astype(jnp.float32), d_heads)

    def rotate_all(raw_values, scales):
        return norm_rotate(raw_values, scales, cos_table, sin_table)
    unused, pull = jax.vjp(rotate_all, queries_raw, gain_query)
    d_queries, grad_query = pull(jnp.transpose(d_queries_rot, (1, 0, 2)))
    unused, pull = jax.vjp(rotate_all, keys_raw, gain_key)
    d_keys, grad_key = pull(d_keys_rot[:, None, :])
    d_queries = d_queries.reshape(length, HQ * HD).astype(jnp.bfloat16)
    d_keys = d_keys.reshape(length, HD).astype(jnp.bfloat16)
    d_values = d_values.astype(jnp.bfloat16)
    q_grad = jnp.dot(d_queries.T, normed_in, preferred_element_type=jnp.float32)
    k_grad = jnp.dot(d_keys.T, normed_in, preferred_element_type=jnp.float32)
    v_grad = jnp.dot(d_values.T, normed_in, preferred_element_type=jnp.float32)
    d_normed_in = jnp.dot(d_queries, w_query, preferred_element_type=jnp.float32) + jnp.dot(d_keys, w_key, preferred_element_type=jnp.float32) + jnp.dot(d_values, w_value, preferred_element_type=jnp.float32)
    unused, pull = jax.vjp(rms_scale, seq_inputs, gain_in)
    d_in_norm, grad_in = pull(d_normed_in)
    input_grad = d_middle + d_in_norm
    gains_grad = jnp.concatenate([grad_in, grad_attn, grad_pre, grad_post, grad_query, grad_key])
    return (output, input_grad, (q_grad, k_grad, v_grad, o_grad, gate_grad, up_grad, down_grad, gains_grad))

def reference(inputs, positions, cotangent, q_weight, k_weight, v_weight, o_weight, gate_weight, up_weight, down_weight, norm_gains):
    weights = (q_weight, k_weight, v_weight, o_weight, gate_weight, up_weight, down_weight)
    gains_all = norm_gains.astype(jnp.float32)

    def seq_step(totals, sliced):
        seq_inputs, seq_positions, seq_cotangent = sliced
        output, input_grad, grads = one_sequence(seq_inputs, seq_cotangent, seq_positions, weights, gains_all)
        totals = tuple((left + right for left, right in zip(totals, grads)))
        return (totals, (output, input_grad))
    empty_sums = tuple((jnp.zeros(weight.shape, jnp.float32) for weight in weights)) + (jnp.zeros(gains_all.shape, jnp.float32),)
    totals, stacked = lax.scan(seq_step, empty_sums, (inputs, positions, cotangent))
    return (stacked[0], stacked[1], totals[0], totals[1], totals[2], totals[3], totals[4], totals[5], totals[6], totals[7])
```

```python
import functools

import jax
import jax.numpy as jnp
from jax import lax
from jax.experimental import pallas as pl
from jax.experimental.pallas import tpu as pltpu
from jax.sharding import PartitionSpec as P

D = 640
HQ = 4
HD = 256
WIN = 512


EPSILON = 1e-06


def shifted(block, axis, distance):
    devices = range(lax.axis_size(axis))
    route = [(i - distance, i) for i in devices if i - distance in devices]
    return lax.ppermute(block, axis, route)


def rms_scale(values, scales):
    inverse = lax.rsqrt(jnp.mean(values * values, axis=-1, keepdims=True) + EPSILON)
    return values * inverse * scales


def rotary_tables(positions):
    half_size = HD // 2
    frequency = 10000.0 ** (-2.0 * jnp.arange(half_size, dtype=jnp.float32) / HD)
    angles = positions.astype(jnp.float32)[:, None] * frequency[None, :]
    angles = jnp.concatenate([angles, angles], axis=-1)
    return (jnp.cos(angles), jnp.sin(angles))


def norm_rotate(raw_values, scales, cos_table, sin_table):
    normed = rms_scale(raw_values, scales)
    front_half = normed[..., : HD // 2]
    back_half = normed[..., HD // 2 :]
    turned = jnp.concatenate([-back_half, front_half], axis=-1)
    return normed * cos_table[:, None, :] + turned * sin_table[:, None, :]


def window_mask(query_pos, key_pos, query_idx, key_idx):
    spacing = query_pos[:, None] - key_pos[None, :]
    return (spacing == query_idx[:, None] - key_idx[None, :]) & (spacing >= 0) & (spacing < WIN)


def glu_product(gate_pre, up_pre):
    return jax.nn.gelu(gate_pre, approximate=True) * up_pre


def split_gains(gains_all):
    return (
        gains_all[0:D],
        gains_all[D : 2 * D],
        gains_all[2 * D : 3 * D],
        gains_all[3 * D : 4 * D],
        gains_all[4 * D : 4 * D + HD],
        gains_all[4 * D + HD : 4 * D + 2 * HD],
    )


def times_rows(left, weight):
    return lax.dot_general(
        left, weight, (((1,), (1,)), ((), ())), preferred_element_type=jnp.float32
    )


def times_plain(left, weight):
    return jnp.dot(left, weight, preferred_element_type=jnp.float32)


def outer_sum(left, right):
    return lax.dot_general(
        left, right, (((0,), (0,)), ((), ())), preferred_element_type=jnp.float32
    )


def score_rows(query_rows, key_rows, allowed, factor):
    raw_scores = factor * times_rows(query_rows, key_rows)
    by_head = raw_scores.reshape(-1, allowed.shape[0], allowed.shape[1])
    return jnp.where(allowed[None], by_head, -1e30).reshape(raw_scores.shape)


MESH_ID = pl.DeviceIdType.MESH
AXIS_Z, AXIS_Y, AXIS_CORE, AXIS_X = range(4)
GATHER_ORDERS = (
    (AXIS_Z, AXIS_Y, AXIS_X, AXIS_CORE),
    (AXIS_Z, AXIS_X, AXIS_Y, AXIS_CORE),
)
SCATTER_ORDERS = (
    (AXIS_CORE, AXIS_X, AXIS_Y, AXIS_Z),
    (AXIS_CORE, AXIS_Y, AXIS_X, AXIS_Z),
)


def grid_sizes(dp_size, seq_size):
    return (dp_size // 4, 2, 2, seq_size)


def own_place():
    dp_index = lax.axis_index("dp")
    return (dp_index // 4, (dp_index // 2) % 2, dp_index % 2, lax.axis_index("seq"))


def peer_place(place, axis, size, hop):
    moved = list(place)
    moved[axis] = (place[axis] + hop) % size
    return tuple(moved)


def device_of(place):
    return ((place[AXIS_Z] * 2 + place[AXIS_Y]) * 2 + place[AXIS_CORE], place[AXIS_X])


def greet(place, sizes):
    barrier = pltpu.get_barrier_semaphore()
    count = 0
    for axis, size in enumerate(sizes):
        for hop in range(1, size):
            pl.semaphore_signal(
                barrier,
                inc=1,
                device_id=device_of(peer_place(place, axis, size, hop)),
                device_id_type=MESH_ID,
            )
            count += 1
    pl.semaphore_wait(barrier, count)


def slot_table(order, sizes):
    slots = {}
    for axis in order:
        for hop in range(1, sizes[axis]):
            slots[(axis, hop)] = len(slots)
    return slots


def gather_kernel(sizes, orders, *refs):
    count = len(orders)
    shards, wholes = refs[:count], refs[count : 2 * count]
    local_sem, send_sem, recv_sem = refs[2 * count :]
    place = own_place()
    tables = [slot_table(order, sizes) for order in orders]

    def block(ref, held):
        return ref.at[tuple(slice(None) if a in held else place[a] for a in range(4))]

    def start(i, stage):
        axis = orders[i][stage]
        held = orders[i][:stage]
        copies = []
        for hop in range(1, sizes[axis]):
            slot = tables[i][(axis, hop)]
            copies.append(
                pltpu.make_async_remote_copy(
                    src_ref=block(wholes[i], held) if stage else shards[i],
                    dst_ref=block(wholes[i], held),
                    send_sem=send_sem.at[i, slot],
                    recv_sem=recv_sem.at[i, slot],
                    device_id=device_of(peer_place(place, axis, sizes[axis], hop)),
                    device_id_type=MESH_ID,
                )
            )
        for copy in copies:
            copy.start()
        return copies

    own = [
        pltpu.make_async_copy(shards[i], block(wholes[i], ()), local_sem.at[i])
        for i in range(count)
    ]
    for copy in own:
        copy.start()
    greet(place, sizes)
    flying = [[start(i, 0)] for i in range(count)]
    for tick in range(count + 3):
        for stage in range(4):
            i = tick - stage
            if not 0 <= i < count:
                continue
            if stage == 0:
                own[i].wait()
            for copy in flying[i][stage]:
                copy.wait()
            if stage < 3:
                flying[i].append(start(i, stage + 1))


def gather_all(sizes, orders, shards):
    count = len(shards)
    slots = sum(size - 1 for size in sizes)
    return pl.pallas_call(
        functools.partial(gather_kernel, sizes, orders),
        out_shape=[jax.ShapeDtypeStruct(sizes + s.shape, s.dtype) for s in shards],
        in_specs=[pl.BlockSpec(memory_space=pl.ANY)] * count,
        out_specs=[pl.BlockSpec(memory_space=pl.ANY)] * count,
        scratch_shapes=[
            pltpu.SemaphoreType.DMA((count,)),
            pltpu.SemaphoreType.DMA((count, slots)),
            pltpu.SemaphoreType.DMA((count, slots)),
        ],
        compiler_params=pltpu.CompilerParams(collective_id=0, has_side_effects=True),
        name="gather_all",
    )(*shards)


def scatter_kernel(sizes, orders, *refs):
    count = len(orders)
    terms, outs = refs[:count], refs[count : 2 * count]
    buffers = refs[2 * count : 9 * count]
    local_sem, send_sem, recv_sem = refs[9 * count :]
    place = own_place()
    tables = [slot_table(order, sizes) for order in orders]
    partial = [list(buffers[7 * i : 7 * i + 3]) for i in range(count)]
    landing = [list(buffers[7 * i + 3 : 7 * i + 7]) for i in range(count)]

    def pick(ref, axes, axis, index):
        return ref.at[tuple(index if a == axis else slice(None) for a in axes)]

    def remaining(i, stage):
        return [a for a in range(4) if a not in orders[i][:stage]]

    def source(i, stage):
        return partial[i][stage - 1] if stage else terms[i]

    def start(i, stage):
        axis = orders[i][stage]
        axes = remaining(i, stage)
        copies = []
        for hop in range(1, sizes[axis]):
            slot = tables[i][(axis, hop)]
            peer = peer_place(place, axis, sizes[axis], hop)
            copies.append(
                pltpu.make_async_remote_copy(
                    src_ref=pick(source(i, stage), axes, axis, peer[axis]),
                    dst_ref=landing[i][stage].at[hop - 1],
                    send_sem=send_sem.at[i, slot],
                    recv_sem=recv_sem.at[i, slot],
                    device_id=device_of(peer),
                    device_id_type=MESH_ID,
                )
            )
        for copy in copies:
            copy.start()
        return copies

    def reduce(i, stage):
        axis = orders[i][stage]
        axes = remaining(i, stage)
        rest = [a for a in axes if a != axis]
        target = partial[i][stage] if stage < 3 else outs[i]
        steps = 1
        for a in rest:
            steps *= sizes[a]

        def body(step, carry):
            index = []
            left = step
            for a in reversed(rest):
                index.insert(0, left % sizes[a])
                left = left // sizes[a]
            by_axis = dict(zip(rest, index))
            if stage:
                mine = source(i, stage)[
                    tuple(place[axis] if a == axis else by_axis[a] for a in axes)
                ]
            else:
                mine = target[tuple(index)]
            total = mine.astype(jnp.float32)
            for hop in range(1, sizes[axis]):
                total += landing[i][stage][(hop - 1, *index)].astype(jnp.float32)
            if stage < 3:
                target[tuple(index)] = total.astype(target.dtype)
            else:
                target[...] = total
            return carry

        if steps == 1:
            body(0, 0)
        else:
            lax.fori_loop(0, steps, body, 0)

    own = [
        pltpu.make_async_copy(
            pick(terms[i], range(4), orders[i][0], place[orders[i][0]]),
            partial[i][0],
            local_sem.at[i],
        )
        for i in range(count)
    ]
    for copy in own:
        copy.start()
    greet(place, sizes)
    flying = [[start(i, 0)] for i in range(count)]
    for tick in range(count + 3):
        for stage in range(4):
            i = tick - stage
            if not 0 <= i < count:
                continue
            if stage == 0:
                own[i].wait()
            for copy in flying[i][stage]:
                copy.wait()
            reduce(i, stage)
            if stage < 3:
                flying[i].append(start(i, stage + 1))


def scatter_sum(sizes, orders, terms):
    count = len(terms)
    slots = sum(size - 1 for size in sizes)
    buffers = []
    for order, term in zip(orders, terms):
        tile = term.shape[4:]
        partial, landing = [], []
        for stage, axis in enumerate(order):
            rest = tuple(sizes[a] for a in range(4) if a not in order[: stage + 1])
            if stage < 3:
                partial.append(pltpu.VMEM(rest + tile, term.dtype))
            landing.append(pltpu.VMEM((max(sizes[axis] - 1, 1),) + rest + tile, term.dtype))
        buffers.extend(partial + landing)
    return pl.pallas_call(
        functools.partial(scatter_kernel, sizes, orders),
        out_shape=[jax.ShapeDtypeStruct(t.shape[4:], jnp.float32) for t in terms],
        in_specs=[pl.BlockSpec(memory_space=pl.ANY)] * count,
        out_specs=[pl.BlockSpec(memory_space=pltpu.VMEM)] * count,
        scratch_shapes=buffers
        + [
            pltpu.SemaphoreType.DMA((count,)),
            pltpu.SemaphoreType.DMA((count, slots)),
            pltpu.SemaphoreType.DMA((count, slots)),
        ],
        compiler_params=pltpu.CompilerParams(
            collective_id=1, has_side_effects=True, vmem_limit_bytes=44 * 1024 * 1024
        ),
        name="scatter_sum",
    )(*terms)


def on_device(
    inputs,
    positions,
    cotangent,
    q_weight,
    k_weight,
    v_weight,
    o_weight,
    gate_weight,
    up_weight,
    down_weight,
    norm_gains,
):
    tokens_here = inputs.shape[1]
    scale = HD ** (-0.5)
    block_index = lax.axis_index("seq")
    sizes = grid_sizes(lax.axis_size("dp"), lax.axis_size("seq"))
    devices = lax.axis_size(("dp", "seq"))
    width_query = q_weight.shape[0]
    width_key = k_weight.shape[0]
    width_ffn = gate_weight.shape[0]
    gain_share = norm_gains.shape[0]
    gain_tile = jnp.pad(norm_gains[None], ((0, 15), (0, -gain_share % 128)))
    first, second = GATHER_ORDERS
    all_gains, w_query, w_kv, w_out, w_upper, w_gate, w_down = gather_all(
        sizes,
        (second, first, second, first, second, first, second),
        (
            gain_tile,
            q_weight,
            jnp.concatenate([k_weight, v_weight], axis=0),
            o_weight,
            up_weight,
            gate_weight,
            down_weight,
        ),
    )
    w_query, w_out, w_upper, w_gate, w_down = [
        w.reshape(-1, D) for w in (w_query, w_out, w_upper, w_gate, w_down)
    ]
    w_kv = w_kv.reshape(devices, 2 * width_key, D)
    w_key = w_kv[:, :width_key].reshape(-1, D)
    w_value = w_kv[:, width_key:].reshape(-1, D)
    gain_in, gain_attn, gain_pre, gain_post, gain_query, gain_key = split_gains(
        all_gains.reshape(devices, 16, -1)[:, 0, :gain_share].reshape(-1).astype(jnp.float32)
    )
    seq_inputs = inputs[0]
    seq_cotangent = cotangent[0]
    every_pos = positions[0]
    own_pos = lax.dynamic_slice_in_dim(every_pos, block_index * tokens_here, tokens_here)
    prior_pos = lax.dynamic_slice_in_dim(
        every_pos, jnp.maximum(block_index - 1, 0) * tokens_here, tokens_here
    )
    query_idx = block_index * tokens_here + jnp.arange(tokens_here, dtype=jnp.int32)
    key_idx = (block_index - 1) * tokens_here + jnp.arange(2 * tokens_here, dtype=jnp.int32)
    allowed = window_mask(own_pos, jnp.concatenate([prior_pos, own_pos]), query_idx, key_idx)
    allowed = allowed & (key_idx >= 0)[None, :]
    cos_table, sin_table = rotary_tables(own_pos)
    normed_in = rms_scale(seq_inputs, gain_in).astype(jnp.bfloat16)
    queries_raw = times_rows(normed_in, w_query).reshape(tokens_here, HQ, HD)
    keys_raw = times_rows(normed_in, w_key).reshape(tokens_here, 1, HD)
    values_raw = times_rows(normed_in, w_value)
    queries_rot = norm_rotate(queries_raw, gain_query, cos_table, sin_table).astype(jnp.bfloat16)
    keys_rot = norm_rotate(keys_raw, gain_key, cos_table, sin_table)[:, 0].astype(jnp.bfloat16)
    values_b = values_raw.astype(jnp.bfloat16)
    prior_keys, prior_values = shifted((keys_rot, values_b), "seq", 1)
    key_rows = jnp.concatenate([prior_keys, keys_rot], axis=0)
    value_rows = jnp.concatenate([prior_values, values_b], axis=0)
    query_rows = jnp.transpose(queries_rot, (1, 0, 2)).reshape(HQ * tokens_here, HD)
    scores = score_rows(query_rows, key_rows, allowed, scale)
    highest = jnp.max(scores, axis=-1, keepdims=True)
    log_total = highest + jnp.log(jnp.sum(jnp.exp(scores - highest), axis=-1, keepdims=True))
    probs_b = jnp.exp(scores - log_total).astype(jnp.bfloat16)
    attended = times_plain(probs_b, value_rows).astype(jnp.bfloat16)
    merged = jnp.transpose(attended.reshape(HQ, tokens_here, HD), (1, 0, 2)).reshape(
        tokens_here, HQ * HD
    )
    branch = times_plain(merged, w_out)
    middle = seq_inputs + rms_scale(branch, gain_attn)
    normed_ff = rms_scale(middle, gain_pre).astype(jnp.bfloat16)
    gate_pre = times_rows(normed_ff, w_gate)
    up_pre = times_rows(normed_ff, w_upper)
    hidden = glu_product(gate_pre, up_pre).astype(jnp.bfloat16)
    ffn_out = times_plain(hidden, w_down)
    output = middle + rms_scale(ffn_out, gain_post)
    unused, pull = jax.vjp(rms_scale, ffn_out, gain_post)
    d_ffn, grad_post = pull(seq_cotangent)
    d_ffn = d_ffn.astype(jnp.bfloat16)
    d_hidden = times_rows(d_ffn, w_down)
    unused, pull = jax.vjp(glu_product, gate_pre, up_pre)
    d_gate, d_up = pull(d_hidden)
    d_gate = d_gate.astype(jnp.bfloat16)
    d_up = d_up.astype(jnp.bfloat16)
    d_normed_ff = times_plain(d_gate, w_gate) + times_plain(d_up, w_upper)
    unused, pull = jax.vjp(rms_scale, middle, gain_pre)
    d_mid_norm, grad_pre = pull(d_normed_ff)
    d_middle = seq_cotangent + d_mid_norm
    unused, pull = jax.vjp(rms_scale, branch, gain_attn)
    d_branch, grad_attn = pull(d_middle)
    d_branch = d_branch.astype(jnp.bfloat16)
    d_merged = times_rows(d_branch, w_out).astype(jnp.bfloat16)
    d_rows = jnp.transpose(d_merged.reshape(tokens_here, HQ, HD), (1, 0, 2)).reshape(
        HQ * tokens_here, HD
    )
    probs = jnp.exp(score_rows(query_rows, key_rows, allowed, scale) - log_total)
    probs_again = probs.astype(jnp.bfloat16)
    delta = jnp.sum(
        d_rows.astype(jnp.float32) * attended.astype(jnp.float32), axis=-1, keepdims=True
    )
    d_probs = times_rows(d_rows, value_rows)
    d_scores = (probs * (d_probs - delta)).astype(jnp.bfloat16)
    d_query_rows = scale * times_plain(d_scores, key_rows)
    d_key_rows = scale * outer_sum(d_scores, query_rows)
    d_value_rows = outer_sum(probs_again, d_rows)
    sent_keys, sent_values = (
        shifted(d_key_rows[:tokens_here].astype(jnp.bfloat16), "seq", -1).astype(jnp.float32),
        shifted(d_value_rows[:tokens_here].astype(jnp.bfloat16), "seq", -1).astype(jnp.float32),
    )
    d_keys_rot = d_key_rows[tokens_here:] + sent_keys
    d_values = (d_value_rows[tokens_here:] + sent_values).astype(jnp.bfloat16)
    d_queries_rot = jnp.transpose(d_query_rows.reshape(HQ, tokens_here, HD), (1, 0, 2))

    def rotate_all(raw_values, scales):
        return norm_rotate(raw_values, scales, cos_table, sin_table)

    unused, pull = jax.vjp(rotate_all, queries_raw, gain_query)
    d_queries, grad_query = pull(d_queries_rot)
    unused, pull = jax.vjp(rotate_all, keys_raw, gain_key)
    d_keys, grad_key = pull(d_keys_rot[:, None, :])
    d_queries = d_queries.reshape(tokens_here, HQ * HD).astype(jnp.bfloat16)
    d_keys = d_keys.reshape(tokens_here, HD).astype(jnp.bfloat16)
    d_normed_in = (
        times_plain(d_queries, w_query)
        + times_plain(d_keys, w_key)
        + times_plain(d_values, w_value)
    )
    unused, pull = jax.vjp(rms_scale, seq_inputs, gain_in)
    d_in_norm, grad_in = pull(d_normed_in)
    input_grad = d_middle + d_in_norm
    gains_grad = jnp.concatenate([grad_in, grad_attn, grad_pre, grad_post, grad_query, grad_key])

    def grad_term(left, right):
        return outer_sum(left, right).astype(jnp.bfloat16)

    def by_owner(term):
        return term.reshape(sizes + (-1, term.shape[-1]))

    kv_term = jnp.concatenate(
        [
            grad_term(d_keys, normed_in).reshape(devices, width_key, D),
            grad_term(d_values, normed_in).reshape(devices, width_key, D),
        ],
        axis=1,
    )
    gain_term = jnp.pad(
        gains_grad.reshape(devices, 1, gain_share), ((0, 0), (0, 7), (0, -gain_share % 128))
    )
    first, second = SCATTER_ORDERS
    gains_sum, down_sum, gate_sum, up_sum, o_sum, q_sum, kv_sum = scatter_sum(
        sizes,
        (second, first, second, first, second, first, second),
        (
            gain_term.reshape(sizes + gain_term.shape[1:]),
            by_owner(grad_term(hidden, d_ffn)),
            by_owner(grad_term(d_gate, normed_ff)),
            by_owner(grad_term(d_up, normed_ff)),
            by_owner(grad_term(merged, d_branch)),
            by_owner(grad_term(d_queries, normed_in)),
            kv_term.reshape(sizes + kv_term.shape[1:]),
        ),
    )
    results = (
        q_sum,
        kv_sum[:width_key],
        kv_sum[width_key:],
        o_sum,
        gate_sum,
        up_sum,
        down_sum,
        gains_sum[0, :gain_share],
    )
    return (output[None], input_grad[None]) + results


def solution(mesh):
    return jax.shard_map(
        on_device,
        mesh=mesh,
        in_specs=(
            P("dp", "seq", None),
            P("dp", None),
            P("dp", "seq", None),
            P(("dp", "seq"), None),
            P(("dp", "seq"), None),
            P(("dp", "seq"), None),
            P(("dp", "seq"), None),
            P(("dp", "seq"), None),
            P(("dp", "seq"), None),
            P(("dp", "seq"), None),
            P(("dp", "seq")),
        ),
        out_specs=(
            P("dp", "seq", None),
            P("dp", "seq", None),
            P(("dp", "seq"), None),
            P(("dp", "seq"), None),
            P(("dp", "seq"), None),
            P(("dp", "seq"), None),
            P(("dp", "seq"), None),
            P(("dp", "seq"), None),
            P(("dp", "seq"), None),
            P(("dp", "seq")),
        ),
        check_vma=False,
    )
```

```python
import functools

import jax
import jax.numpy as jnp
from jax import lax
from jax.experimental import pallas as pl
from jax.experimental.pallas import tpu as pltpu
from jax.sharding import PartitionSpec as P

D = 640
HQ = 4
HD = 256
WIN = 512


EPSILON = 1e-06


def shifted(block, axis, distance):
    devices = range(lax.axis_size(axis))
    route = [(i - distance, i) for i in devices if i - distance in devices]
    return lax.ppermute(block, axis, route)


def rms_scale(values, scales):
    inverse = lax.rsqrt(jnp.mean(values * values, axis=-1, keepdims=True) + EPSILON)
    return values * inverse * scales


def rotary_tables(positions):
    half_size = HD // 2
    frequency = 10000.0 ** (-2.0 * jnp.arange(half_size, dtype=jnp.float32) / HD)
    angles = positions.astype(jnp.float32)[:, None] * frequency[None, :]
    angles = jnp.concatenate([angles, angles], axis=-1)
    return (jnp.cos(angles), jnp.sin(angles))


def norm_rotate(raw_values, scales, cos_table, sin_table):
    normed = rms_scale(raw_values, scales)
    front_half = normed[..., : HD // 2]
    back_half = normed[..., HD // 2 :]
    turned = jnp.concatenate([-back_half, front_half], axis=-1)
    return normed * cos_table[:, None, :] + turned * sin_table[:, None, :]


def window_mask(query_pos, key_pos, query_idx, key_idx):
    spacing = query_pos[:, None] - key_pos[None, :]
    return (spacing == query_idx[:, None] - key_idx[None, :]) & (spacing >= 0) & (spacing < WIN)


def glu_product(gate_pre, up_pre):
    return jax.nn.gelu(gate_pre, approximate=True) * up_pre


def split_gains(gains_all):
    return (
        gains_all[0:D],
        gains_all[D : 2 * D],
        gains_all[2 * D : 3 * D],
        gains_all[3 * D : 4 * D],
        gains_all[4 * D : 4 * D + HD],
        gains_all[4 * D + HD : 4 * D + 2 * HD],
    )


def lay_end_to_end(parts):
    whole = sum(part.shape[0] for part in parts)
    total, before = 0.0, 0
    for part in parts:
        total += jnp.pad(part, (before, whole - before - part.shape[0]))
        before += part.shape[0]
    return total


def times_rows(left, weight):
    return lax.dot_general(
        left, weight, (((1,), (1,)), ((), ())), preferred_element_type=jnp.float32
    )


def times_plain(left, weight):
    return jnp.dot(left, weight, preferred_element_type=jnp.float32)


def outer_sum(left, right):
    return lax.dot_general(
        left, right, (((0,), (0,)), ((), ())), preferred_element_type=jnp.float32
    )


def score_rows(query_rows, key_rows, allowed, factor):
    raw_scores = factor * times_rows(query_rows, key_rows)
    by_head = raw_scores.reshape(-1, allowed.shape[0], allowed.shape[1])
    return jnp.where(allowed[None], by_head, -1e30).reshape(raw_scores.shape)


MESH_ID = pl.DeviceIdType.MESH
AXIS_Z, AXIS_Y, AXIS_CORE, AXIS_X = range(4)
GATHER_ORDERS = (
    (AXIS_Z, AXIS_Y, AXIS_X, AXIS_CORE),
    (AXIS_Z, AXIS_X, AXIS_Y, AXIS_CORE),
)
SCATTER_ORDERS = (
    (AXIS_CORE, AXIS_X, AXIS_Y, AXIS_Z),
    (AXIS_CORE, AXIS_Y, AXIS_X, AXIS_Z),
)


def grid_sizes(dp_size, seq_size):
    return (dp_size // 4, 2, 2, seq_size)


def own_place():
    dp_index = lax.axis_index("dp")
    return (dp_index // 4, (dp_index // 2) % 2, dp_index % 2, lax.axis_index("seq"))


def peer_place(place, axis, size, hop):
    moved = list(place)
    moved[axis] = (place[axis] + hop) % size
    return tuple(moved)


def device_of(place):
    return ((place[AXIS_Z] * 2 + place[AXIS_Y]) * 2 + place[AXIS_CORE], place[AXIS_X])


def greet(place, sizes):
    barrier = pltpu.get_barrier_semaphore()
    count = 0
    for axis, size in enumerate(sizes):
        for hop in range(1, size):
            pl.semaphore_signal(
                barrier,
                inc=1,
                device_id=device_of(peer_place(place, axis, size, hop)),
                device_id_type=MESH_ID,
            )
            count += 1
    pl.semaphore_wait(barrier, count)


def slot_table(order, sizes):
    slots = {}
    for axis in order:
        for hop in range(1, sizes[axis]):
            slots[(axis, hop)] = len(slots)
    return slots


PIECE_ROWS = 32


def cut_pieces(heights, orders):
    pieces, rows_given = [], [0] * len(orders)
    for array, height in enumerate(heights):
        size = PIECE_ROWS if height % PIECE_ROWS == 0 else height
        for first in range(0, height, size):
            which = rows_given.index(min(rows_given))
            rows_given[which] += size
            pieces.append((array, first, size, orders[which]))
    return pieces


def rows_of(ref, index, piece):
    return ref.at[(*index, pl.ds(piece[1], piece[2]))]


def gather_kernel(sizes, pieces, arrays, *refs):
    count = len(pieces)
    orders = [piece[3] for piece in pieces]
    shards = [refs[piece[0]] for piece in pieces]
    wholes = [refs[arrays + piece[0]] for piece in pieces]
    local_sem, send_sem, recv_sem = refs[2 * arrays :]
    place = own_place()
    tables = [slot_table(order, sizes) for order in orders]

    def block(i, held):
        index = tuple(slice(None) if a in held else place[a] for a in range(4))
        return rows_of(wholes[i], index, pieces[i])

    def start(i, stage):
        axis = orders[i][stage]
        held = orders[i][:stage]
        copies = []
        for hop in range(1, sizes[axis]):
            slot = tables[i][(axis, hop)]
            copies.append(
                pltpu.make_async_remote_copy(
                    src_ref=block(i, held) if stage else rows_of(shards[i], (), pieces[i]),
                    dst_ref=block(i, held),
                    send_sem=send_sem.at[i, slot],
                    recv_sem=recv_sem.at[i, slot],
                    device_id=device_of(peer_place(place, axis, sizes[axis], hop)),
                    device_id_type=MESH_ID,
                )
            )
        for copy in copies:
            copy.start()
        return copies

    own = [
        pltpu.make_async_copy(
            rows_of(shards[i], (), pieces[i]), block(i, ()), local_sem.at[i]
        )
        for i in range(count)
    ]
    for copy in own:
        copy.start()
    greet(place, sizes)
    flying = [[start(i, 0)] for i in range(count)]
    for tick in range(count + 3):
        for stage in range(4):
            i = tick - stage
            if not 0 <= i < count:
                continue
            if stage == 0:
                own[i].wait()
            for copy in flying[i][stage]:
                copy.wait()
            if stage < 3:
                flying[i].append(start(i, stage + 1))


def gather_all(sizes, shards):
    pieces = cut_pieces([s.shape[0] for s in shards], GATHER_ORDERS)
    arrays, count = len(shards), len(pieces)
    slots = sum(size - 1 for size in sizes)
    return pl.pallas_call(
        functools.partial(gather_kernel, sizes, pieces, arrays),
        out_shape=[jax.ShapeDtypeStruct(sizes + s.shape, s.dtype) for s in shards],
        in_specs=[pl.BlockSpec(memory_space=pl.ANY)] * arrays,
        out_specs=[pl.BlockSpec(memory_space=pl.ANY)] * arrays,
        scratch_shapes=[
            pltpu.SemaphoreType.DMA((count,)),
            pltpu.SemaphoreType.DMA((count, slots)),
            pltpu.SemaphoreType.DMA((count, slots)),
        ],
        compiler_params=pltpu.CompilerParams(collective_id=0, has_side_effects=True),
        name="gather_all",
    )(*shards)


def scatter_kernel(sizes, pieces, arrays, *refs):
    count = len(pieces)
    orders = [piece[3] for piece in pieces]
    terms = [refs[piece[0]] for piece in pieces]
    outs = [rows_of(refs[arrays + piece[0]], (), piece) for piece in pieces]
    buffers = refs[2 * arrays : 2 * arrays + 7 * count]
    local_sem, send_sem, recv_sem = refs[2 * arrays + 7 * count :]
    place = own_place()
    tables = [slot_table(order, sizes) for order in orders]
    partial = [list(buffers[7 * i : 7 * i + 3]) for i in range(count)]
    landing = [list(buffers[7 * i + 3 : 7 * i + 7]) for i in range(count)]

    def pick(i, stage, axes, axis, index):
        where = tuple(index if a == axis else slice(None) for a in axes)
        if stage:
            return partial[i][stage - 1].at[where]
        return rows_of(terms[i], where, pieces[i])

    def remaining(i, stage):
        return [a for a in range(4) if a not in orders[i][:stage]]

    def start(i, stage):
        axis = orders[i][stage]
        axes = remaining(i, stage)
        copies = []
        for hop in range(1, sizes[axis]):
            slot = tables[i][(axis, hop)]
            peer = peer_place(place, axis, sizes[axis], hop)
            copies.append(
                pltpu.make_async_remote_copy(
                    src_ref=pick(i, stage, axes, axis, peer[axis]),
                    dst_ref=landing[i][stage].at[hop - 1],
                    send_sem=send_sem.at[i, slot],
                    recv_sem=recv_sem.at[i, slot],
                    device_id=device_of(peer),
                    device_id_type=MESH_ID,
                )
            )
        for copy in copies:
            copy.start()
        return copies

    def reduce(i, stage):
        axis = orders[i][stage]
        axes = remaining(i, stage)
        rest = [a for a in axes if a != axis]
        target = partial[i][stage] if stage < 3 else outs[i]
        steps = 1
        for a in rest:
            steps *= sizes[a]

        def body(step, carry):
            index = []
            left = step
            for a in reversed(rest):
                index.insert(0, left % sizes[a])
                left = left // sizes[a]
            by_axis = dict(zip(rest, index))
            if stage:
                mine = partial[i][stage - 1][
                    tuple(place[axis] if a == axis else by_axis[a] for a in axes)
                ]
            else:
                mine = target[tuple(index)]
            total = mine.astype(jnp.float32)
            for hop in range(1, sizes[axis]):
                total += landing[i][stage][(hop - 1, *index)].astype(jnp.float32)
            if stage < 3:
                target[tuple(index)] = total.astype(target.dtype)
            else:
                target[...] = total
            return carry

        if steps == 1:
            body(0, 0)
        else:
            lax.fori_loop(0, steps, body, 0)

    own = [
        pltpu.make_async_copy(
            pick(i, 0, range(4), orders[i][0], place[orders[i][0]]),
            partial[i][0],
            local_sem.at[i],
        )
        for i in range(count)
    ]
    for copy in own:
        copy.start()
    greet(place, sizes)
    flying = [[start(i, 0)] for i in range(count)]
    for tick in range(count + 3):
        for stage in range(4):
            i = tick - stage
            if not 0 <= i < count:
                continue
            if stage == 0:
                own[i].wait()
            for copy in flying[i][stage]:
                copy.wait()
            reduce(i, stage)
            if stage < 3:
                flying[i].append(start(i, stage + 1))


def scatter_sum(sizes, terms):
    pieces = cut_pieces([t.shape[4] for t in terms], SCATTER_ORDERS)
    arrays, count = len(terms), len(pieces)
    slots = sum(size - 1 for size in sizes)
    buffers = []
    for array, _, height, order in pieces:
        term = terms[array]
        tile = (height, term.shape[5])
        partial, landing = [], []
        for stage, axis in enumerate(order):
            rest = tuple(sizes[a] for a in range(4) if a not in order[: stage + 1])
            if stage < 3:
                partial.append(pltpu.VMEM(rest + tile, term.dtype))
            landing.append(pltpu.VMEM((max(sizes[axis] - 1, 1),) + rest + tile, term.dtype))
        buffers.extend(partial + landing)
    return pl.pallas_call(
        functools.partial(scatter_kernel, sizes, pieces, arrays),
        out_shape=[jax.ShapeDtypeStruct(t.shape[4:], jnp.float32) for t in terms],
        in_specs=[pl.BlockSpec(memory_space=pl.ANY)] * arrays,
        out_specs=[pl.BlockSpec(memory_space=pltpu.VMEM)] * arrays,
        scratch_shapes=buffers
        + [
            pltpu.SemaphoreType.DMA((count,)),
            pltpu.SemaphoreType.DMA((count, slots)),
            pltpu.SemaphoreType.DMA((count, slots)),
        ],
        compiler_params=pltpu.CompilerParams(
            collective_id=1, has_side_effects=True, vmem_limit_bytes=44 * 1024 * 1024
        ),
        name="scatter_sum",
    )(*terms)


def on_device(
    inputs,
    positions,
    cotangent,
    q_weight,
    k_weight,
    v_weight,
    o_weight,
    gate_weight,
    up_weight,
    down_weight,
    norm_gains,
):
    tokens_here = inputs.shape[1]
    scale = HD ** (-0.5)
    block_index = lax.axis_index("seq")
    sizes = grid_sizes(lax.axis_size("dp"), lax.axis_size("seq"))
    devices = lax.axis_size(("dp", "seq"))
    width_query = q_weight.shape[0]
    width_key = k_weight.shape[0]
    width_ffn = gate_weight.shape[0]
    gain_share = norm_gains.shape[0]
    gain_tile = jnp.pad(norm_gains[None], ((0, 15), (0, -gain_share % 128)))
    all_gains, w_query, w_kv, w_out, w_upper, w_gate, w_down = gather_all(
        sizes,
        (
            gain_tile,
            q_weight,
            jnp.concatenate([k_weight, v_weight], axis=0),
            o_weight,
            up_weight,
            gate_weight,
            down_weight,
        ),
    )
    w_query, w_out, w_upper, w_gate, w_down = [
        w.reshape(-1, D) for w in (w_query, w_out, w_upper, w_gate, w_down)
    ]
    w_kv = w_kv.reshape(devices, 2 * width_key, D)
    w_key = w_kv[:, :width_key].reshape(-1, D)
    w_value = w_kv[:, width_key:].reshape(-1, D)
    gain_in, gain_attn, gain_pre, gain_post, gain_query, gain_key = split_gains(
        all_gains.reshape(devices, 16, -1)[:, 0, :gain_share].reshape(-1).astype(jnp.float32)
    )
    seq_inputs = inputs[0]
    seq_cotangent = cotangent[0]
    every_pos = positions[0]
    own_pos = lax.dynamic_slice_in_dim(every_pos, block_index * tokens_here, tokens_here)
    prior_pos = lax.dynamic_slice_in_dim(
        every_pos, jnp.maximum(block_index - 1, 0) * tokens_here, tokens_here
    )
    query_idx = block_index * tokens_here + jnp.arange(tokens_here, dtype=jnp.int32)
    key_idx = (block_index - 1) * tokens_here + jnp.arange(2 * tokens_here, dtype=jnp.int32)
    allowed = window_mask(own_pos, jnp.concatenate([prior_pos, own_pos]), query_idx, key_idx)
    allowed = allowed & (key_idx >= 0)[None, :]
    cos_table, sin_table = rotary_tables(own_pos)
    normed_in = rms_scale(seq_inputs, gain_in).astype(jnp.bfloat16)
    queries_raw = times_rows(normed_in, w_query).reshape(tokens_here, HQ, HD)
    keys_raw = times_rows(normed_in, w_key).reshape(tokens_here, 1, HD)
    values_raw = times_rows(normed_in, w_value)
    queries_rot = norm_rotate(queries_raw, gain_query, cos_table, sin_table).astype(jnp.bfloat16)
    keys_rot = norm_rotate(keys_raw, gain_key, cos_table, sin_table)[:, 0].astype(jnp.bfloat16)
    values_b = values_raw.astype(jnp.bfloat16)
    prior_keys, prior_values = shifted((keys_rot, values_b), "seq", 1)
    key_rows = jnp.concatenate([prior_keys, keys_rot], axis=0)
    value_rows = jnp.concatenate([prior_values, values_b], axis=0)
    query_rows = jnp.transpose(queries_rot, (1, 0, 2)).reshape(HQ * tokens_here, HD)
    scores = score_rows(query_rows, key_rows, allowed, scale)
    highest = jnp.max(scores, axis=-1, keepdims=True)
    log_total = highest + jnp.log(jnp.sum(jnp.exp(scores - highest), axis=-1, keepdims=True))
    probs_b = jnp.exp(scores - log_total).astype(jnp.bfloat16)
    attended = times_plain(probs_b, value_rows).astype(jnp.bfloat16)
    merged = jnp.transpose(attended.reshape(HQ, tokens_here, HD), (1, 0, 2)).reshape(
        tokens_here, HQ * HD
    )
    branch = times_plain(merged, w_out)
    middle = seq_inputs + rms_scale(branch, gain_attn)
    normed_ff = rms_scale(middle, gain_pre).astype(jnp.bfloat16)
    gate_pre = times_rows(normed_ff, w_gate)
    up_pre = times_rows(normed_ff, w_upper)
    hidden = glu_product(gate_pre, up_pre).astype(jnp.bfloat16)
    ffn_out = times_plain(hidden, w_down)
    output = middle + rms_scale(ffn_out, gain_post)
    unused, pull = jax.vjp(rms_scale, ffn_out, gain_post)
    d_ffn, grad_post = pull(seq_cotangent)
    d_ffn = d_ffn.astype(jnp.bfloat16)
    d_hidden = times_rows(d_ffn, w_down)
    unused, pull = jax.vjp(glu_product, gate_pre, up_pre)
    d_gate, d_up = pull(d_hidden)
    d_gate = d_gate.astype(jnp.bfloat16)
    d_up = d_up.astype(jnp.bfloat16)
    d_normed_ff = times_plain(d_gate, w_gate) + times_plain(d_up, w_upper)
    unused, pull = jax.vjp(rms_scale, middle, gain_pre)
    d_mid_norm, grad_pre = pull(d_normed_ff)
    d_middle = seq_cotangent + d_mid_norm
    unused, pull = jax.vjp(rms_scale, branch, gain_attn)
    d_branch, grad_attn = pull(d_middle)
    d_branch = d_branch.astype(jnp.bfloat16)
    d_merged = times_rows(d_branch, w_out).astype(jnp.bfloat16)
    d_rows = jnp.transpose(d_merged.reshape(tokens_here, HQ, HD), (1, 0, 2)).reshape(
        HQ * tokens_here, HD
    )
    probs = jnp.exp(score_rows(query_rows, key_rows, allowed, scale) - log_total)
    probs_again = probs.astype(jnp.bfloat16)
    delta = jnp.sum(
        d_rows.astype(jnp.float32) * attended.astype(jnp.float32), axis=-1, keepdims=True
    )
    d_probs = times_rows(d_rows, value_rows)
    d_scores = (probs * (d_probs - delta)).astype(jnp.bfloat16)
    d_query_rows = scale * times_plain(d_scores, key_rows)
    d_key_rows = scale * outer_sum(d_scores, query_rows)
    d_value_rows = outer_sum(probs_again, d_rows)
    sent_keys, sent_values = (
        shifted(d_key_rows[:tokens_here].astype(jnp.bfloat16), "seq", -1).astype(jnp.float32),
        shifted(d_value_rows[:tokens_here].astype(jnp.bfloat16), "seq", -1).astype(jnp.float32),
    )
    d_keys_rot = d_key_rows[tokens_here:] + sent_keys
    d_values = (d_value_rows[tokens_here:] + sent_values).astype(jnp.bfloat16)
    d_queries_rot = jnp.transpose(d_query_rows.reshape(HQ, tokens_here, HD), (1, 0, 2))

    def rotate_all(raw_values, scales):
        return norm_rotate(raw_values, scales, cos_table, sin_table)

    unused, pull = jax.vjp(rotate_all, queries_raw, gain_query)
    d_queries, grad_query = pull(d_queries_rot)
    unused, pull = jax.vjp(rotate_all, keys_raw, gain_key)
    d_keys, grad_key = pull(d_keys_rot[:, None, :])
    d_queries = d_queries.reshape(tokens_here, HQ * HD).astype(jnp.bfloat16)
    d_keys = d_keys.reshape(tokens_here, HD).astype(jnp.bfloat16)
    d_normed_in = (
        times_plain(d_queries, w_query)
        + times_plain(d_keys, w_key)
        + times_plain(d_values, w_value)
    )
    unused, pull = jax.vjp(rms_scale, seq_inputs, gain_in)
    d_in_norm, grad_in = pull(d_normed_in)
    input_grad = d_middle + d_in_norm
    gains_grad = lay_end_to_end([grad_in, grad_attn, grad_pre, grad_post, grad_query, grad_key])

    def grad_term(left, right):
        return outer_sum(left, right).astype(jnp.bfloat16)

    def by_owner(term):
        return term.reshape(sizes + (-1, term.shape[-1]))

    kv_term = jnp.concatenate(
        [
            grad_term(d_keys, normed_in).reshape(devices, width_key, D),
            grad_term(d_values, normed_in).reshape(devices, width_key, D),
        ],
        axis=1,
    )
    gain_term = jnp.pad(
        gains_grad.reshape(devices, 1, gain_share), ((0, 0), (0, 7), (0, -gain_share % 128))
    )
    gains_sum, down_sum, gate_sum, up_sum, o_sum, q_sum, kv_sum = scatter_sum(
        sizes,
        (
            gain_term.reshape(sizes + gain_term.shape[1:]),
            by_owner(grad_term(hidden, d_ffn)),
            by_owner(grad_term(d_gate, normed_ff)),
            by_owner(grad_term(d_up, normed_ff)),
            by_owner(grad_term(merged, d_branch)),
            by_owner(grad_term(d_queries, normed_in)),
            kv_term.reshape(sizes + kv_term.shape[1:]),
        ),
    )
    results = (
        q_sum,
        kv_sum[:width_key],
        kv_sum[width_key:],
        o_sum,
        gate_sum,
        up_sum,
        down_sum,
        gains_sum[0, :gain_share],
    )
    return (output[None], input_grad[None]) + results


def solution(mesh):
    return jax.shard_map(
        on_device,
        mesh=mesh,
        in_specs=(
            P("dp", "seq", None),
            P("dp", None),
            P("dp", "seq", None),
            P(("dp", "seq"), None),
            P(("dp", "seq"), None),
            P(("dp", "seq"), None),
            P(("dp", "seq"), None),
            P(("dp", "seq"), None),
            P(("dp", "seq"), None),
            P(("dp", "seq"), None),
            P(("dp", "seq")),
        ),
        out_specs=(
            P("dp", "seq", None),
            P("dp", "seq", None),
            P(("dp", "seq"), None),
            P(("dp", "seq"), None),
            P(("dp", "seq"), None),
            P(("dp", "seq"), None),
            P(("dp", "seq"), None),
            P(("dp", "seq"), None),
            P(("dp", "seq"), None),
            P(("dp", "seq")),
        ),
        check_vma=False,
    )
```
